256 devices in a mesh: blk: 16 (over z_lo, x, core), eng: 16 (over z_hi, y).
Axes of the slice: x: 4, y: 4, z: 8 (z_hi: 4, z_lo: 2; z = z_hi * 2 + z_lo), core: 2. Of those that a mesh axis runs over, the one named last changes fastest.
Arguments:
- g_lesser: bfloat16 [64, 16, 2, 256, 256], P('eng', 'blk'), may hold values from -6 to 6
- g_greater: bfloat16 [64, 16, 2, 256, 256], P('eng', 'blk'), may hold values from -6 to 6
- coulomb: bfloat16 [16, 2, 256, 256], P('blk'), may hold values from -0.21875 to 0.21875
- coupling: int32 [16], P('blk'), may hold values 0 or 1
- lag_slots: int32 [64], replicated, may hold values from 0 to 63
Outputs:
- sigma_lesser: bfloat16 [64, 16, 2, 256, 256], P('eng', 'blk')
- sigma_greater: bfloat16 [64, 16, 2, 256, 256], P('eng', 'blk')
The draws below stay inside these ranges and needn't reach their ends.
Inputs may be any that keep to these rules, and one draw needn't show every extreme that they name: `lag_slots`: offsets may repeat across slots.
All inputs are finite; a program needn't handle non-finite values. No bound on the sum of `coupling` on one device may be relied on, other than what follows from the above.
Results may differ from the reference program's by a relative error of at most 0.0065.
Values may be sent and summed in bfloat16 or wider, within the bound.
No kernel may reach another device: no remote copies, remote signals or barrier semaphores. Data moves between devices by JAX's collectives and lax.ppermute only.
A program may use at most 128 MiB of HBM per device.

```python
import jax
import jax.numpy as jnp
from jax import lax

BS = 256
NB = 16
NE = 64


def touch_ends(result, rng, least, top_value):
    longest = result.shape.index(max(result.shape))
    spots = []
    for shift in (0, 1):
        where = [jax.random.randint(jax.random.fold_in(rng, axis), (), 0, length) for axis, length in enumerate(result.shape)]
        where[longest] = (where[longest] + shift) % result.shape[longest]
        spots.append(tuple(where))
    return result.at[spots[0]].set(least).at[spots[1]].set(top_value)


def levels(own_key, shape, pieces, smallest, largest):
    gain, own = 1.0, jax.random.fold_in(own_key, 6)
    for position, shards_of in pieces:
        steps = jnp.exp(jax.random.uniform(jax.random.fold_in(own, position), (shards_of,), jnp.float32, smallest / len(pieces), largest / len(pieces)))
        gain = gain * jnp.repeat(steps, shape[position] // shards_of).reshape([-1 if axis == position else 1 for axis in range(len(shape))])
    return gain


def bell_draw(rng, shape, spread, bound, pieces=(), held_as=jnp.bfloat16):
    factor_of = levels(rng, shape, pieces, -0.22, 0.18) if pieces else 1.0
    entries = jax.random.normal(rng, shape, jnp.float32) * spread * factor_of
    return jnp.minimum(jnp.maximum(entries, -bound), bound).astype(held_as)


def setup_inputs(seed: int = 0) -> dict:
    splits = jax.random.split(jax.random.key(seed), 6)
    g_lesser = bell_draw(splits[0], (NE, NB, 2, BS, BS), 1.0, 6.0, ((0, 16), (1, 16)))
    g_greater = bell_draw(splits[1], (NE, NB, 2, BS, BS), 1.0, 6.0, ((0, 16), (1, 16)))
    coulomb = bell_draw(splits[2], (NB, 2, BS, BS), (3 * BS) ** -0.5, 0.21875, ((0, 16),))
    coupling = touch_ends((jax.random.randint(splits[3], (NB,), 0, 4) < 3).astype(jnp.int32), jax.random.fold_in(splits[3], 1), 0, 1)
    lag_slots = touch_ends(jax.random.randint(splits[4], (NE,), 0, NE), jax.random.fold_in(splits[4], 1), 0, NE - 1).astype(jnp.int32)
    return dict(g_lesser=g_lesser, g_greater=g_greater, coulomb=coulomb, coupling=coupling, lag_slots=lag_slots)


def product(einsum_form, left_side, right_side):
    return jnp.einsum(einsum_form, left_side.astype(jnp.float32), right_side.astype(jnp.float32), precision=lax.Precision.HIGHEST)


def screen(pad_p, pad_v):
    row_count = pad_v.shape[0] - 2
    v_diag_zero = pad_v[1:row_count + 1, 0]
    v_diag_plus = pad_v[2:, 0]
    v_up_minus = pad_v[:row_count, 1]
    v_up_zero = pad_v[1:row_count + 1, 1]
    v_up_plus = pad_v[2:, 1]
    p_diag_minus = pad_p[:, :row_count, 0]
    p_diag_zero = pad_p[:, 1:row_count + 1, 0]
    p_diag_plus = pad_p[:, 2:, 0]
    p_up_minus = pad_p[:, :row_count, 1]
    p_up_zero = pad_p[:, 1:row_count + 1, 1]
    p_up_plus = pad_p[:, 2:, 1]
    q_minus = (product("rba,krbc->krac", v_up_minus, p_diag_minus) + product("rab,krcb->krac", v_diag_zero, p_up_minus)).astype(jnp.bfloat16)
    q_zero = (product("rba,krbc->krac", v_up_minus, p_up_minus) + product("rab,krbc->krac", v_diag_zero, p_diag_zero) + product("rab,krcb->krac", v_up_zero, p_up_zero)).astype(jnp.bfloat16)
    q_plus = (product("rab,krbc->krac", v_diag_zero, p_up_zero) + product("rab,krbc->krac", v_up_zero, p_diag_plus)).astype(jnp.bfloat16)
    q_far = product("rab,krbc->krac", v_up_zero, p_up_plus).astype(jnp.bfloat16)
    w_diag = product("krab,rbc->krac", q_minus, v_up_minus) + product("krab,rbc->krac", q_zero, v_diag_zero) + product("krab,rcb->krac", q_plus, v_up_zero)
    w_upper = product("krab,rbc->krac", q_zero, v_up_zero) + product("krab,rbc->krac", q_plus, v_diag_plus) + product("krab,rcb->krac", q_far, v_up_plus)
    return jnp.stack([w_diag, w_upper], axis=2).astype(jnp.bfloat16)


def reference(g_lesser, g_greater, coulomb, coupling, lag_slots):
    norm_factor = NE ** -0.5

    def polar_row(kind_pair):
        lesser = kind_pair[0].astype(jnp.float32)
        greater = kind_pair[1].astype(jnp.float32)
        f_lesser = jnp.fft.rfft(lesser, axis=0)
        f_greater = jnp.fft.rfft(greater, axis=0)
        c_lesser = jnp.fft.irfft(f_lesser * jnp.conj(f_greater), n=NE, axis=0)
        c_greater = jnp.fft.irfft(f_greater * jnp.conj(f_lesser), n=NE, axis=0)
        return ((c_lesser[lag_slots] * norm_factor).astype(jnp.bfloat16), (c_greater[lag_slots] * norm_factor).astype(jnp.bfloat16))

    by_rows = (jnp.moveaxis(g_lesser, 1, 0), jnp.moveaxis(g_greater, 1, 0))
    p_lesser, p_greater = lax.map(polar_row, by_rows)
    polarization = jnp.stack([jnp.moveaxis(p_lesser, 0, 1), jnp.moveaxis(p_greater, 0, 1)], axis=1)

    row_ids = jnp.arange(NB, dtype=jnp.int32)
    kept_links = (coupling * (row_ids < NB - 1).astype(jnp.int32)).astype(jnp.bfloat16)
    v_both = jnp.stack([coulomb[:, 0], coulomb[:, 1] * kept_links[:, None, None]], axis=1)
    pad_v = jnp.pad(v_both, ((1, 1), (0, 0), (0, 0), (0, 0)))

    def screen_energy(kind_pair):
        return screen(jnp.pad(kind_pair, ((0, 0), (1, 1), (0, 0), (0, 0), (0, 0))), pad_v)

    screened = lax.map(screen_energy, polarization)
    w_rows_lesser = jnp.moveaxis(screened[:, 0], 1, 0)
    w_rows_greater = jnp.moveaxis(screened[:, 1], 1, 0)

    def convolve_kind(green_part, screened_part):
        placed = jnp.zeros(screened_part.shape, jnp.float32).at[lag_slots].add(screened_part.astype(jnp.float32))
        spectrum = jnp.fft.rfft(green_part.astype(jnp.float32), axis=0) * jnp.fft.rfft(placed, axis=0)
        return (jnp.fft.irfft(spectrum, n=NE, axis=0) * norm_factor).astype(jnp.bfloat16)

    def self_row(row_data):
        return (convolve_kind(row_data[0], row_data[2]), convolve_kind(row_data[1], row_data[3]))

    s_lesser, s_greater = lax.map(self_row, (by_rows[0], by_rows[1], w_rows_lesser, w_rows_greater))
    return (jnp.moveaxis(s_lesser, 0, 1), jnp.moveaxis(s_greater, 0, 1))
```

```python
import jax
import jax.numpy as jnp
import numpy as np
from jax import lax
from jax.experimental import pallas as pl
from jax.experimental.pallas import tpu as pltpu
from jax.sharding import PartitionSpec as P

BF = jnp.bfloat16
F32 = jnp.float32


def real_tables(n):
    h = n // 2
    f = np.arange(h)[:, None]
    k = np.arange(n)[None, :]
    ang = 2.0 * np.pi * (f * k % n) / n
    re = np.cos(ang)
    im = -np.sin(ang)
    im[0] = np.cos(np.pi * k[0])
    fwd = np.concatenate([re, im], 0)
    w = np.full((2 * h, 1), 2.0)
    w[0] = 1.0
    w[h] = 1.0
    inv = (fwd * w).T / n
    return fwd.astype(np.float32), inv.astype(np.float32)


def split2(x):
    hi = x.astype(BF)
    lo = (x - hi.astype(F32)).astype(BF)
    return hi, lo


def dot(a, b):
    return jnp.dot(a, b, preferred_element_type=F32)


def forward(tab, x):
    n = tab.shape[0]
    hi, lo = split2(tab)
    both = dot(jnp.concatenate([hi, lo], 0), x)
    return both[:n] + both[n:]


def backward(tab, re, im):
    hi, lo = split2(tab)
    xh, xl = split2(jnp.concatenate([re, im], 0))
    return dot(jnp.concatenate([hi, hi, lo], 1), jnp.concatenate([xh, xl, xh], 0))


def corr_kernel(fwd_ref, inv_ref, l_ref, g_ref, c_ref):
    h = fwd_ref.shape[0] // 2
    fl = forward(fwd_ref[...], l_ref[...])
    fg = forward(fwd_ref[...], g_ref[...])
    lr, li, gr, gi = fl[:h], fl[h:], fg[:h], fg[h:]
    first = lax.broadcasted_iota(jnp.int32, lr.shape, 0) == 0
    rr, ii = lr * gr, li * gi
    re = rr + jnp.where(first, 0.0, ii)
    im = jnp.where(first, ii, li * gr - lr * gi)
    c_ref[...] = backward(inv_ref[...], re, im).astype(c_ref.dtype)


def conv_kernel(fwd_ref, lag_ref, inv_ref, g_ref, d_ref, s_ref):
    h = fwd_ref.shape[0] // 2
    fg = forward(fwd_ref[...], g_ref[...])
    fd = forward(lag_ref[0], d_ref[...])
    gr, gi, dr, di = fg[:h], fg[h:], fd[:h], fd[h:]
    first = lax.broadcasted_iota(jnp.int32, gr.shape, 0) == 0
    rr, ii = gr * dr, gi * di
    re = rr - jnp.where(first, 0.0, ii)
    im = jnp.where(first, ii, gr * di + gi * dr)
    s_ref[...] = backward(inv_ref[...], re, im).astype(s_ref.dtype)


def dot_t(a, b):
    return lax.dot_general(a, b, (((1,), (1,)), ((), ())), preferred_element_type=F32)


def t_dot(a, b):
    return lax.dot_general(a, b, (((0,), (0,)), ((), ())), preferred_element_type=F32)


def screen_kernel(vm_ref, v0_ref, vp_ref, pm_ref, p0_ref, pp_ref, w_ref):
    def block(ref, j):
        x = ref[:, j]
        return x.reshape(x.shape[0] * x.shape[1], x.shape[2])

    vum, vd0, vu0 = block(vm_ref, 1), block(v0_ref, 0), block(v0_ref, 1)
    vdp, vup = block(vp_ref, 0), block(vp_ref, 1)
    dm, um = block(pm_ref, 0), block(pm_ref, 1)
    d0, u0 = block(p0_ref, 0), block(p0_ref, 1)
    dp, up = block(pp_ref, 0), block(pp_ref, 1)
    q_minus = (t_dot(vum, dm) + dot_t(vd0, um)).astype(BF)
    q_zero = (t_dot(vum, um) + dot(vd0, d0) + dot_t(vu0, u0)).astype(BF)
    q_plus = (dot(vd0, u0) + dot(vu0, dp)).astype(BF)
    q_far = dot(vu0, up).astype(BF)
    w_diag = dot(q_minus, vum) + dot(q_zero, vd0) + dot_t(q_plus, vu0)
    w_up = dot(q_zero, vu0) + dot(q_plus, vdp) + dot_t(q_far, vup)
    shape = w_ref.shape[:1] + w_ref.shape[2:]
    w_ref[:, 0] = w_diag.astype(w_ref.dtype).reshape(shape)
    w_ref[:, 1] = w_up.astype(w_ref.dtype).reshape(shape)


def full(a):
    return pl.BlockSpec(a.shape, lambda *_: (0,) * a.ndim)


def correlate(fwd, inv, flat, tile):
    n, both = flat.shape
    tiles = both // 2 // tile
    return pl.pallas_call(
        corr_kernel,
        grid=(tiles,),
        in_specs=[
            full(fwd),
            full(inv),
            pl.BlockSpec((n, tile), lambda j: (0, j)),
            pl.BlockSpec((n, tile), lambda j: (0, j + tiles)),
        ],
        out_specs=pl.BlockSpec((n, tile), lambda j: (0, j)),
        out_shape=jax.ShapeDtypeStruct((n, both // 2), BF),
        name="corr",
    )(fwd, inv, flat, flat)


def convolve(fwd, lag_tabs, inv, flat, d, tile):
    n, both = flat.shape
    tiles = both // 2 // tile
    return pl.pallas_call(
        conv_kernel,
        grid=(2, tiles),
        in_specs=[
            full(fwd),
            pl.BlockSpec((1,) + lag_tabs.shape[1:], lambda s, j: (s, 0, 0)),
            full(inv),
            pl.BlockSpec((n, tile), lambda s, j: (0, s * tiles + j)),
            pl.BlockSpec((n, tile), lambda s, j: (0, j)),
        ],
        out_specs=pl.BlockSpec((n, tile), lambda s, j: (0, s * tiles + j)),
        out_shape=jax.ShapeDtypeStruct((n, both), BF),
        name="conv",
    )(fwd, lag_tabs, inv, flat, d)


def screen(stack, before, after, count):
    r, _, t, s, b = stack.shape
    one = (r, None, t, s, b)

    def at(k):
        return pl.BlockSpec(one, lambda j: (0, k, 0, 0, 0))

    def each():
        return pl.BlockSpec(one, lambda j: (0, j, 0, 0, 0))

    return pl.pallas_call(
        screen_kernel,
        grid=(count,),
        in_specs=[at(count), at(count), at(count), each(), each(), each()],
        out_specs=each(),
        out_shape=jax.ShapeDtypeStruct((r, count, t, s, b), BF),
        name="screen",
    )(before, stack, after, before, stack, after)


def exchange(x):
    return lax.all_to_all(x, "eng", split_axis=0, concat_axis=0, tiled=True)


def on_device(g_lesser, g_greater, coulomb, coupling, lag_slots):
    parts = lax.axis_size("eng")
    blocks = lax.axis_size("blk")
    own, _, two, bs, _ = g_lesser.shape
    energies = own * parts
    slab = bs // parts
    norm = energies ** (-0.5)
    fwd_np, inv_np = real_tables(energies)
    fwd = jnp.asarray(fwd_np)
    inv = jnp.asarray(inv_np * np.float32(norm))
    back_ids = (-np.arange(energies)) % energies
    ids = jnp.arange(energies, dtype=jnp.int32)
    cnt = jnp.sum((lag_slots[:, None] == ids[None, :]).astype(F32), axis=0)
    cnt_neg = jnp.sum((lag_slots[:, None] == jnp.asarray(back_ids, jnp.int32)[None, :]).astype(F32), axis=0)
    lag_tabs = jnp.stack([fwd * cnt[None], jnp.asarray(fwd_np[:, back_ids]) * cnt_neg[None]])

    both = jnp.stack([g_lesser[:, 0], g_greater[:, 0]], axis=1)
    both = both.reshape(own, 2, two, parts, slab, bs).transpose(3, 0, 1, 2, 4, 5)
    el = exchange(both).reshape(energies, 2 * two * slab * bs)
    tile = two * slab * bs // 4
    c = correlate(fwd, inv, el, tile)
    p = exchange(c.reshape(parts, own, two, slab, bs))

    row = lax.axis_index("blk")
    kept = (coupling[0] * (row < blocks - 1).astype(jnp.int32)).astype(BF)
    v_both = jnp.stack([coulomb[0, 0], coulomb[0, 1] * kept], axis=0)
    v_both = v_both.reshape(two, parts, 1, slab, bs).transpose(1, 2, 0, 3, 4)
    stack = jnp.concatenate([p, v_both], axis=1)
    ups = [(i, i + 1) for i in range(blocks - 1)]
    before = lax.ppermute(stack, "blk", ups)
    after = lax.ppermute(stack, "blk", [(j, i) for i, j in ups])
    w = screen(stack, before, after, own)

    d = exchange(w).reshape(energies, two * slab * bs)
    s = convolve(fwd, lag_tabs, inv, el, d, tile)
    s = exchange(s.reshape(parts, own, 2, two, slab, bs))
    s = s.transpose(1, 2, 3, 0, 4, 5).reshape(own, 2, 1, two, bs, bs)
    return (s[:, 0], s[:, 1])


def solution(mesh):
    spec = P("eng", "blk", None, None, None)
    return jax.shard_map(
        on_device,
        mesh=mesh,
        in_specs=(spec, spec, P("blk", None, None, None), P("blk"), P()),
        out_specs=(spec, spec),
        check_vma=False,
    )
```

```python
import jax
import jax.numpy as jnp
import numpy as np
from jax import lax
from jax.experimental import pallas as pl
from jax.experimental.pallas import tpu as pltpu
from jax.sharding import PartitionSpec as P

BF = jnp.bfloat16
F32 = jnp.float32


def real_tables(n):
    h = n // 2
    f = np.arange(h)[:, None]
    k = np.arange(n)[None, :]
    ang = 2.0 * np.pi * (f * k % n) / n
    re = np.cos(ang)
    im = -np.sin(ang)
    im[0] = np.cos(np.pi * k[0])
    fwd = np.concatenate([re, im], 0)
    w = np.full((2 * h, 1), 2.0)
    w[0] = 1.0
    w[h] = 1.0
    inv = (fwd * w).T / n
    return fwd.astype(np.float32), inv.astype(np.float32)


def split2(x):
    hi = x.astype(BF)
    lo = (x - hi.astype(F32)).astype(BF)
    return hi, lo


def dot(a, b):
    return jnp.dot(a, b, preferred_element_type=F32)


def wide_forward(tab):
    return jnp.concatenate(split2(tab), 1)


def forward(wide, x):
    return dot(wide, jnp.concatenate([x, x], 0))


def wide_backward(tab):
    hi, lo = split2(tab)
    return jnp.concatenate([hi, hi, lo], 1)


def backward(wide, re, im):
    xh, xl = split2(jnp.concatenate([re, im], 0))
    return dot(wide, jnp.concatenate([xh, xl, xh], 0))


def corr_kernel(fwd_ref, inv_ref, x_ref, c_ref):
    h = fwd_ref.shape[0] // 2
    columns = c_ref.shape[1]
    fwd = wide_forward(fwd_ref[...])
    fl = forward(fwd, x_ref[:, :columns])
    fg = forward(fwd, x_ref[:, columns:])
    lr, li, gr, gi = fl[:h], fl[h:], fg[:h], fg[h:]
    first = lax.broadcasted_iota(jnp.int32, lr.shape, 0) == 0
    ii = li * gi
    re = lr * gr + jnp.where(first, 0.0, ii)
    im = jnp.where(first, ii, li * gr - lr * gi)
    c_ref[...] = backward(wide_backward(inv_ref[...]), re, im).astype(c_ref.dtype)


def conv_kernel(fwd_ref, lag_ref, inv_ref, g_ref, d_ref, s_ref):
    h = fwd_ref.shape[0] // 2
    columns = d_ref.shape[1]
    fwd = wide_forward(fwd_ref[...])
    inv = wide_backward(inv_ref[...])
    for kind in range(2):
        here = slice(kind * columns, (kind + 1) * columns)
        fg = forward(fwd, g_ref[:, here])
        fd = forward(wide_forward(lag_ref[kind]), d_ref[...])
        gr, gi, dr, di = fg[:h], fg[h:], fd[:h], fd[h:]
        first = lax.broadcasted_iota(jnp.int32, gr.shape, 0) == 0
        ii = gi * di
        re = gr * dr - jnp.where(first, 0.0, ii)
        im = jnp.where(first, ii, gr * di + gi * dr)
        s_ref[:, here] = backward(inv, re, im).astype(s_ref.dtype)


def screen_kernel(m_ref, z_ref, p_ref, w_ref):
    own = w_ref.shape[1]

    def block(ref, k, j):
        x = ref[:, k, j]
        return x.reshape(x.shape[0] * x.shape[1], x.shape[2])

    def rows(*xs):
        return jnp.concatenate(xs, 0)

    def cols(*xs):
        return jnp.concatenate(xs, 1)

    vum, vd0, vu0 = block(m_ref, own, 1), block(z_ref, own, 0), block(z_ref, own, 1)
    vdp, vup = block(p_ref, own, 0), block(p_ref, own, 1)
    left = cols(vum.T, vd0, vu0)
    right_diag = rows(vum, vd0, vu0.T)
    right_up = rows(vu0, vdp, vup.T)
    n = vd0.shape[0]
    shape = (w_ref.shape[0],) + w_ref.shape[3:]
    for k in range(own):
        dm, um = block(m_ref, k, 0), block(m_ref, k, 1)
        d0, u0 = block(z_ref, k, 0), block(z_ref, k, 1)
        dp, up = block(p_ref, k, 0), block(p_ref, k, 1)
        q_minus = dot(left[:, : 2 * n], rows(dm, um.T)).astype(BF)
        q_zero = dot(left, rows(um, d0, u0.T)).astype(BF)
        q_plus = dot(left[:, n:], rows(u0, dp)).astype(BF)
        q_far = dot(left[:, 2 * n :], up).astype(BF)
        w_diag = dot(cols(q_minus, q_zero, q_plus), right_diag)
        w_up = dot(cols(q_zero, q_plus, q_far), right_up)
        w_ref[:, k, 0] = w_diag.astype(w_ref.dtype).reshape(shape)
        w_ref[:, k, 1] = w_up.astype(w_ref.dtype).reshape(shape)


def local_call(kernel, out_shape, name, *operands):
    vmem = pl.BlockSpec(memory_space=pltpu.VMEM)
    return pl.pallas_call(
        kernel,
        in_specs=[vmem] * len(operands),
        out_specs=vmem,
        out_shape=pltpu.VMEM(out_shape, BF),
        compiler_params=pltpu.CompilerParams(vmem_limit_bytes=40 * 2**20),
        name=name,
    )(*[pltpu.with_memory_space_constraint(x, pltpu.VMEM) for x in operands])


def exchange(x):
    return lax.all_to_all(x, "eng", split_axis=0, concat_axis=0, tiled=True)


def on_device(g_lesser, g_greater, coulomb, coupling, lag_slots):
    parts = lax.axis_size("eng")
    blocks = lax.axis_size("blk")
    own, _, two, bs, _ = g_lesser.shape
    energies = own * parts
    slab = bs // parts
    norm = energies ** (-0.5)
    fwd_np, inv_np = real_tables(energies)
    fwd = jnp.asarray(fwd_np)
    inv = jnp.asarray(inv_np * np.float32(norm))
    back_ids = (-np.arange(energies)) % energies
    ids = jnp.arange(energies, dtype=jnp.int32)
    cnt = jnp.sum((lag_slots[:, None] == ids[None, :]).astype(F32), axis=0)
    cnt_neg = jnp.sum((lag_slots[:, None] == jnp.asarray(back_ids, jnp.int32)[None, :]).astype(F32), axis=0)
    lag_tabs = jnp.stack([fwd * cnt[None], jnp.asarray(fwd_np[:, back_ids]) * cnt_neg[None]])

    both = jnp.stack([g_lesser[:, 0], g_greater[:, 0]], axis=1)
    both = both.reshape(own, 2, two, parts, slab, bs).transpose(3, 0, 1, 2, 4, 5)
    el = exchange(both).reshape(energies, 2 * two * slab * bs)
    columns = two * slab * bs
    c = local_call(corr_kernel, (energies, columns), "corr", fwd, inv, el)

    row = lax.axis_index("blk")
    kept = (coupling[0] * (row < blocks - 1).astype(jnp.int32)).astype(BF)
    v_both = jnp.stack([coulomb[0, 0], coulomb[0, 1] * kept], axis=0)
    v_both = v_both.reshape(two, parts, 1, slab, bs).transpose(1, 2, 0, 3, 4)
    p = exchange(c.reshape(parts, own, two, slab, bs))
    stack = jnp.concatenate([p, v_both], axis=1)
    ups = [(i, i + 1) for i in range(blocks - 1)]
    before = lax.ppermute(stack, "blk", ups)
    after = lax.ppermute(stack, "blk", [(j, i) for i, j in ups])
    w = local_call(screen_kernel, p.shape, "screen", before, stack, after)

    d = exchange(w).reshape(energies, columns)
    s = local_call(conv_kernel, el.shape, "conv", fwd, lag_tabs, inv, el, d)
    s = exchange(s.reshape(parts, own, 2, two, slab, bs))
    s = s.transpose(1, 2, 3, 0, 4, 5).reshape(own, 2, 1, two, bs, bs)
    return (s[:, 0], s[:, 1])


def solution(mesh):
    spec = P("eng", "blk", None, None, None)
    return jax.shard_map(
        on_device,
        mesh=mesh,
        in_specs=(spec, spec, P("blk", None, None, None), P("blk"), P()),
        out_specs=(spec, spec),
        check_vma=False,
    )
```

```python
import jax
import jax.numpy as jnp
import numpy as np
from jax import lax
from jax.experimental import pallas as pl
from jax.experimental.pallas import tpu as pltpu
from jax.sharding import PartitionSpec as P

BF = jnp.bfloat16
F32 = jnp.float32
MIB = 2**20

FIRST = 20000
SECOND = 10000


def real_tables(n):
    h = n // 2
    f = np.arange(h)[:, None]
    k = np.arange(n)[None, :]
    ang = 2.0 * np.pi * (f * k % n) / n
    re = np.cos(ang)
    im = -np.sin(ang)
    im[0] = np.cos(np.pi * k[0])
    fwd = np.concatenate([re, im], 0)
    w = np.full((2 * h, 1), 2.0)
    w[0] = 1.0
    w[h] = 1.0
    inv = (fwd * w).T / n
    return fwd.astype(np.float32), inv.astype(np.float32)


def split2(x):
    hi = x.astype(BF)
    lo = (x - hi.astype(F32)).astype(BF)
    return hi, lo


def dot(a, b):
    return jnp.dot(a, b, preferred_element_type=F32)


def wide_forward(tab):
    return jnp.concatenate(split2(tab), 1)


def forward(wide, x):
    return dot(wide, jnp.concatenate([x, x], 0))


def wide_backward(tab):
    hi, lo = split2(tab)
    return jnp.concatenate([hi, hi, lo], 1)


def backward(wide, re, im):
    xh, xl = split2(jnp.concatenate([re, im], 0))
    return dot(wide, jnp.concatenate([xh, xl, xh], 0))


def corr_kernel(fwd_ref, inv_ref, x_ref, c_ref):
    h = fwd_ref.shape[0] // 2
    columns = c_ref.shape[1]
    fwd = wide_forward(fwd_ref[...])
    fl = forward(fwd, x_ref[:, :columns])
    fg = forward(fwd, x_ref[:, columns:])
    lr, li, gr, gi = fl[:h], fl[h:], fg[:h], fg[h:]
    first = lax.broadcasted_iota(jnp.int32, lr.shape, 0) == 0
    ii = li * gi
    re = lr * gr + jnp.where(first, 0.0, ii)
    im = jnp.where(first, ii, li * gr - lr * gi)
    c_ref[...] = backward(wide_backward(inv_ref[...]), re, im).astype(c_ref.dtype)


def conv_kernel(fwd_ref, lag_ref, inv_ref, g_ref, d_ref, s_ref):
    h = fwd_ref.shape[0] // 2
    columns = d_ref.shape[1]
    fwd = wide_forward(fwd_ref[...])
    inv = wide_backward(inv_ref[...])
    for kind in range(2):
        here = slice(kind * columns, (kind + 1) * columns)
        fg = forward(fwd, g_ref[:, here])
        fd = forward(wide_forward(lag_ref[kind]), d_ref[...])
        gr, gi, dr, di = fg[:h], fg[h:], fd[:h], fd[h:]
        first = lax.broadcasted_iota(jnp.int32, gr.shape, 0) == 0
        ii = gi * di
        re = gr * dr - jnp.where(first, 0.0, ii)
        im = jnp.where(first, ii, gr * di + gi * dr)
        s_ref[:, here] = backward(inv, re, im).astype(s_ref.dtype)


def screen_kernel(m_ref, z_ref, p_ref, w_ref):
    own = w_ref.shape[1]
    take_turn(SECOND)

    def block(ref, k, j):
        x = ref[:, k, j]
        return x.reshape(x.shape[0] * x.shape[1], x.shape[2])

    def rows(*xs):
        return jnp.concatenate(xs, 0)

    def cols(*xs):
        return jnp.concatenate(xs, 1)

    vum, vd0, vu0 = block(m_ref, own, 1), block(z_ref, own, 0), block(z_ref, own, 1)
    vdp, vup = block(p_ref, own, 0), block(p_ref, own, 1)
    left = cols(vum.T, vd0, vu0)
    right_diag = rows(vum, vd0, vu0.T)
    right_up = rows(vu0, vdp, vup.T)
    n = vd0.shape[0]
    shape = (w_ref.shape[0],) + w_ref.shape[3:]
    for k in range(own):
        dm, um = block(m_ref, k, 0), block(m_ref, k, 1)
        d0, u0 = block(z_ref, k, 0), block(z_ref, k, 1)
        dp, up = block(p_ref, k, 0), block(p_ref, k, 1)
        q_minus = dot(left[:, : 2 * n], rows(dm, um.T)).astype(BF)
        q_zero = dot(left, rows(um, d0, u0.T)).astype(BF)
        q_plus = dot(left[:, n:], rows(u0, dp)).astype(BF)
        q_far = dot(left[:, 2 * n :], up).astype(BF)
        w_diag = dot(cols(q_minus, q_zero, q_plus), right_diag)
        w_up = dot(cols(q_zero, q_plus, q_far), right_up)
        w_ref[:, k, 0] = w_diag.astype(w_ref.dtype).reshape(shape)
        w_ref[:, k, 1] = w_up.astype(w_ref.dtype).reshape(shape)


VMEM = pl.BlockSpec(memory_space=pltpu.VMEM)
HBM = pl.BlockSpec(memory_space=pltpu.HBM)


def local_call(kernel, out_shape, name, *operands, near=True, mib=32):
    return pl.pallas_call(
        kernel,
        in_specs=[VMEM] * len(operands),
        out_specs=VMEM if near else VMEM,
        out_shape=pltpu.VMEM(out_shape, BF) if near else jax.ShapeDtypeStruct(out_shape, BF),
        compiler_params=pltpu.CompilerParams(vmem_limit_bytes=mib * MIB),
        name=name,
    )(*[pltpu.with_memory_space_constraint(x, pltpu.VMEM) for x in operands])


def far(x):
    return pltpu.with_memory_space_constraint(x, pltpu.HBM)


def take_turn(nanos):
    @pl.when(lax.axis_index("blk") % 2 == 1)
    def _():
        pl.delay(nanos)


def run_all(copies):
    for c in copies:
        c.start()
    return copies


def pack_kernel(l_ref, g_ref, o_ref, sems):
    parts, slab = o_ref.shape[0], o_ref.shape[4]
    copies = run_all(
        [
            pltpu.make_async_copy(
                ref.at[:, 0, :, pl.ds(q * slab, slab), :], o_ref.at[q, :, kind], sems.at[kind, q]
            )
            for q in range(parts)
            for kind, ref in enumerate((l_ref, g_ref))
        ]
    )
    take_turn(FIRST)
    for c in copies:
        c.wait()


def pack(g_lesser, g_greater, parts):
    own, _, two, bs, _ = g_lesser.shape
    return pl.pallas_call(
        pack_kernel,
        in_specs=[HBM, HBM],
        out_specs=VMEM,
        out_shape=pltpu.VMEM((parts, own, 2, two, bs // parts, bs), BF),
        scratch_shapes=[pltpu.SemaphoreType.DMA((2, parts))],
        compiler_params=pltpu.CompilerParams(vmem_limit_bytes=8 * MIB),
        name="pack",
    )(far(g_lesser), far(g_greater))


def unpack_kernel(s_ref, l_ref, g_ref, sems):
    parts, slab = s_ref.shape[0], s_ref.shape[4]
    copies = run_all(
        [
            pltpu.make_async_copy(
                s_ref.at[q, :, kind], ref.at[:, 0, :, pl.ds(q * slab, slab), :], sems.at[kind, q]
            )
            for q in range(parts)
            for kind, ref in enumerate((l_ref, g_ref))
        ]
    )
    for c in copies:
        c.wait()


def unpack(s):
    parts, own, _, two, slab, bs = s.shape
    out = jax.ShapeDtypeStruct((own, 1, two, bs, bs), BF)
    return pl.pallas_call(
        unpack_kernel,
        in_specs=[VMEM],
        out_specs=[HBM, HBM],
        out_shape=[out, out],
        scratch_shapes=[pltpu.SemaphoreType.DMA((2, parts))],
        compiler_params=pltpu.CompilerParams(vmem_limit_bytes=8 * MIB),
        name="unpack",
    )(pltpu.with_memory_space_constraint(s, pltpu.VMEM))


def exchange(x):
    return lax.all_to_all(x, "eng", split_axis=0, concat_axis=0, tiled=True)


def on_device(g_lesser, g_greater, coulomb, coupling, lag_slots):
    parts = lax.axis_size("eng")
    blocks = lax.axis_size("blk")
    own, _, two, bs, _ = g_lesser.shape
    energies = own * parts
    slab = bs // parts
    norm = energies ** (-0.5)
    fwd_np, inv_np = real_tables(energies)
    fwd = jnp.asarray(fwd_np)
    inv = jnp.asarray(inv_np * np.float32(norm))
    back_ids = (-np.arange(energies)) % energies
    ids = jnp.arange(energies, dtype=jnp.int32)
    cnt = jnp.sum((lag_slots[:, None] == ids[None, :]).astype(F32), axis=0)
    cnt_neg = jnp.sum((lag_slots[:, None] == jnp.asarray(back_ids, jnp.int32)[None, :]).astype(F32), axis=0)
    lag_tabs = jnp.stack([fwd * cnt[None], jnp.asarray(fwd_np[:, back_ids]) * cnt_neg[None]])

    row = lax.axis_index("blk")
    el = exchange(pack(g_lesser, g_greater, parts)).reshape(energies, 2 * two * slab * bs)
    columns = two * slab * bs
    c = local_call(corr_kernel, (energies, columns), "corr", fwd, inv, el)

    kept = (coupling[0] * (row < blocks - 1).astype(jnp.int32)).astype(BF)
    v_both = jnp.stack([coulomb[0, 0], coulomb[0, 1] * kept], axis=0)
    v_both = v_both.reshape(two, parts, 1, slab, bs).transpose(1, 2, 0, 3, 4)
    p = exchange(c.reshape(parts, own, two, slab, bs))
    stack = jnp.concatenate([p, v_both], axis=1)
    ups = [(i, i + 1) for i in range(blocks - 1)]
    before = lax.ppermute(stack, "blk", ups)
    after = lax.ppermute(stack, "blk", [(j, i) for i, j in ups])
    w = local_call(screen_kernel, p.shape, "screen", before, stack, after, near=False, mib=24)

    d = exchange(w).reshape(energies, columns)
    s = local_call(conv_kernel, el.shape, "conv", fwd, lag_tabs, inv, el, d)
    s = exchange(s.reshape(parts, own, 2, two, slab, bs))
    return tuple(unpack(s))


def solution(mesh):
    spec = P("eng", "blk", None, None, None)
    return jax.shard_map(
        on_device,
        mesh=mesh,
        in_specs=(spec, spec, P("blk", None, None, None), P("blk"), P()),
        out_specs=(spec, spec),
        check_vma=False,
    )
```
